32 devices in a mesh: tm: 1, space: 32 (over z, y, x, core).
Axes of the slice: x: 2, y: 2, z: 4, core: 2. Of those that a mesh axis runs over, the one named last changes fastest.
Arguments:
- vectors: bfloat16 [1, 3, 2, 96, 64, 256], P('tm', None, None, None, 'space'), may hold values from -120 to 120
- links: bfloat16 [1, 3, 3, 3, 2, 64, 256], P('tm', None, None, None, None, 'space'), may hold values from -2.5 to 2.5
- directions: int32 [6], replicated, may hold values from 0 to 3, as said below
- momenta: int32 [6, 3], replicated, may hold values from -2 to 2, as said below
Outputs:
- elementals: float32 [1, 6, 2, 96, 96], P(None, None, None, 'space')
The draws below stay inside these ranges and needn't reach their ends.
Inputs may be any that keep to these rules, and one draw needn't show every extreme that they name: `directions`: each of 0, 1, 2 and 3 appears at least once. `momenta`: the third component is 0, and the first two are never both 0.
All inputs are finite; a program needn't handle non-finite values.
Results may differ from the reference program's by a relative error of at most 0.0027.
Values may be sent and summed in bfloat16 or wider, within the bound.
A program may use at most 128 MiB of HBM per device.

```python
import math
import jax
import jax.numpy as jnp
from jax import lax

NV = 96
NCOMB = 6
LX = 16
LY = 16
NT = 1
NZ = 64


def draw_vectors(key, part):
    key_base, key_scale = jax.random.split(jax.random.fold_in(key, 11))
    shape = (NT, 3, 2, NV, NZ, LX * LY)
    depth = jnp.arange(NZ, dtype=jnp.float32) / max(NZ - 1, 1)
    scales = 10.0 ** jax.random.uniform(key_scale, (NV,), jnp.float32, 0.0, 1.0)
    base = jnp.clip(jax.random.normal(key_base, shape, jnp.float32), -6.0, 6.0)
    envelope = 1.0 + depth
    values = base * scales[None, None, None, :, None, None] * envelope[None, None, None, None, :, None]
    return values.astype(jnp.bfloat16)


def draw_directions(key, part):
    key_extra, key_order = jax.random.split(jax.random.fold_in(key, 23))
    extra = jax.random.randint(key_extra, (NCOMB - 4,), 0, 4).astype(jnp.int32)
    values = jnp.concatenate([jnp.arange(4, dtype=jnp.int32), extra])
    return jax.random.permutation(key_order, values).astype(jnp.int32)


def draw_momenta(key, part):
    plane = jax.random.randint(jax.random.fold_in(key, 37), (NCOMB, 2), -2, 3).astype(jnp.int32)
    both_zero = (plane[:, 0] == 0) & (plane[:, 1] == 0)
    first = jnp.where(both_zero, 1, plane[:, 0]).astype(jnp.int32)
    third = jnp.zeros((NCOMB,), jnp.int32)
    return jnp.stack([first, plane[:, 1], third], axis=1).astype(jnp.int32)


def levels(own_key, dims, cuts, low, largest):
    def one(dim, blocks):
        steps = jax.random.uniform(jax.random.fold_in(jax.random.fold_in(own_key, 6), dim), (blocks,), jnp.float32, low / len(cuts), largest / len(cuts))
        return jnp.repeat(jnp.exp(steps), dims[dim] // blocks).reshape((-1,) + (1,) * (len(dims) - dim - 1))

    gain = one(*cuts[0])
    for cut in cuts[1:]:
        gain = gain * one(*cut)
    return gain


def gaussian(stream_key, dims, spread, limit, pieces=(), kind=jnp.bfloat16):
    entries = spread * jax.random.normal(stream_key, dims, jnp.float32)
    if pieces:
        entries = entries * levels(stream_key, dims, pieces, -0.22, 0.18)
    return jnp.clip(entries, -limit, limit).astype(kind)


def setup_inputs(seed: int = 0) -> dict:
    streams_of = jax.random.split(jax.random.key(seed), 5)
    vectors = draw_vectors(jax.random.fold_in(streams_of[4], 71), 0)
    links = gaussian(streams_of[1], (NT, 3, 3, 3, 2, NZ, LX * LY), 0.4, 2.5, ((5, 32),))
    directions = draw_directions(jax.random.fold_in(streams_of[4], 71), 0)
    momenta = draw_momenta(jax.random.fold_in(streams_of[4], 71), 0)
    return dict(vectors=vectors, links=links, directions=directions, momenta=momenta)


def times_link(link, field):
    link = link.astype(jnp.float32)
    field = field.astype(jnp.float32)
    outputs = []
    for a in range(3):
        total_real = 0.0
        total_imag = 0.0
        for b in range(3):
            link_real = link[a, b, 0]
            link_imag = link[a, b, 1]
            total_real = total_real + link_real * field[b, 0] - link_imag * field[b, 1]
            total_imag = total_imag + link_real * field[b, 1] + link_imag * field[b, 0]
        outputs.append(jnp.stack([total_real, total_imag]))
    return jnp.stack(outputs)

def times_dagger(link, field):
    link = link.astype(jnp.float32)
    field = field.astype(jnp.float32)
    outputs = []
    for a in range(3):
        total_real = 0.0
        total_imag = 0.0
        for b in range(3):
            link_real = link[b, a, 0]
            link_imag = link[b, a, 1]
            total_real = total_real + link_real * field[b, 0] + link_imag * field[b, 1]
            total_imag = total_imag + link_real * field[b, 1] - link_imag * field[b, 0]
        outputs.append(jnp.stack([total_real, total_imag]))
    return jnp.stack(outputs)

def slice_elementals(vectors_t, links_t, directions, momenta):
    field = vectors_t.astype(jnp.float32).reshape(3, 2, NV, NZ, LY, LX)
    link_field = links_t.reshape(3, 3, 3, 2, NZ, LY, LX)
    volume = NZ * LY * LX
    norms = lax.optimization_barrier(jnp.sum(field * field, axis=(0, 1, 3, 4, 5))) / (3.0 * volume)
    scale = 1.0 / (math.sqrt(3.0 * volume) * jnp.sqrt(norms[:, None] * norms[None, :]))
    zpos = jnp.arange(NZ, dtype=jnp.float32)[:, None, None]
    ypos = jnp.arange(LY, dtype=jnp.float32)[None, :, None]
    xpos = jnp.arange(LX, dtype=jnp.float32)[None, None, :]

    def make_branch(mu, axis):

        def branch():
            ahead = times_link(link_field[mu], jnp.roll(field, -1, axis=axis))
            behind = jnp.roll(times_dagger(link_field[mu], field), 1, axis=axis)
            return 0.5 * (ahead - behind)
        return branch
    branches = [lambda: field, make_branch(0, 5), make_branch(1, 4), make_branch(2, 3)]
    flat_field = field.reshape(3, 2, NV, volume)
    results = []
    for k in range(NCOMB):
        displaced = lax.switch(directions[k], branches)
        px = momenta[k, 0].astype(jnp.float32)
        py = momenta[k, 1].astype(jnp.float32)
        pz = momenta[k, 2].astype(jnp.float32)
        angle = 2.0 * math.pi * (px * xpos / LX + py * ypos / LY + pz * zpos / NZ)
        cosine = jnp.cos(angle)
        sine = jnp.sin(angle)
        real_part = displaced[:, 0] * cosine + displaced[:, 1] * sine
        imag_part = displaced[:, 1] * cosine - displaced[:, 0] * sine
        phased = jnp.stack([real_part, imag_part], axis=1).astype(jnp.bfloat16).astype(jnp.float32)
        phased = phased.reshape(3, 2, NV, volume)
        swapped = jnp.concatenate([phased[:, 1:2], -phased[:, 0:1]], axis=1)
        raw_real = jnp.einsum('cris,crjs->ij', flat_field, phased, precision=lax.Precision.HIGHEST)
        raw_imag = jnp.einsum('cris,crjs->ij', flat_field, swapped, precision=lax.Precision.HIGHEST)
        results.append(jnp.stack([raw_real * scale, raw_imag * scale]))
    return jnp.stack(results)

def reference(vectors, links, directions, momenta):

    def one_slice(pair):
        return slice_elementals(pair[0], pair[1], directions, momenta)
    return lax.map(one_slice, (vectors, links))
```

```python
import functools
import math

import jax
import jax.numpy as jnp
from jax import lax
from jax.experimental import pallas as pl
from jax.experimental.pallas import tpu as pltpu
from jax.sharding import PartitionSpec as P

LX = 16
CHUNK = 2
ROWS = 16
MESH = pl.DeviceIdType.MESH


def kernel(
    count, volume, total_z,
    vec_ref, links_ref, directions_ref, momenta_ref,
    out_ref,
    halo, link_halo, lf, shifted, moved, disp, angles, phased, raw, send_a, recv_a, stage, send_b, recv_b, total,
    halo_send, halo_recv, a_send, a_recv, b_send, b_recv,
):
    wide, span = vec_ref.shape
    nv = wide // 2
    sites = links_ref.shape[-1]
    depth = links_ref.shape[-2]
    half = span // depth
    ncomb = directions_ref.shape[0]
    own_rows = nv // count
    groups = count // 2
    per = 2 * own_rows
    chunks = ncomb // CHUNK
    me = lax.axis_index("space")
    core = lax.rem(me, 2)
    group = me // 2
    partner = me + 1 - 2 * core
    up = lax.rem(me + 1, count)
    down = lax.rem(me + count - 1, count)
    other = lax.rem(me + count - 1 + 2 * core, count)

    def peer(step):
        return lax.rem(group + step, groups) * 2 + core

    barrier = pltpu.get_barrier_semaphore()
    for target in [partner, other] + [peer(step) for step in range(1, groups)]:
        pl.semaphore_signal(barrier, inc=1, device_id={"space": target}, device_id_type=MESH)
    pl.semaphore_wait(barrier, groups + 1)

    halo_copies = [
        pltpu.make_async_remote_copy(
            src_ref=vec_ref.at[:, pl.ds(0, half)], dst_ref=halo.at[0],
            send_sem=halo_send.at[0], recv_sem=halo_recv.at[0],
            device_id={"space": down}, device_id_type=MESH,
        ),
        pltpu.make_async_remote_copy(
            src_ref=vec_ref.at[:, pl.ds((depth - 1) * half, half)], dst_ref=halo.at[1],
            send_sem=halo_send.at[1], recv_sem=halo_recv.at[1],
            device_id={"space": up}, device_id_type=MESH,
        ),
        pltpu.make_async_remote_copy(
            src_ref=links_ref.at[2], dst_ref=link_halo,
            send_sem=halo_send.at[2], recv_sem=halo_recv.at[2],
            device_id={"space": up}, device_id_type=MESH,
        ),
    ]
    for copy in halo_copies:
        copy.start()

    for mu in range(3):
        for n in range(18):
            a, b, r = n // 6, (n // 2) % 3, n % 2
            lf[mu, pl.ds(depth * n, depth), :] = 0.5 * links_ref[mu, a, b, r].astype(jnp.float32)
    xlane = lax.broadcasted_iota(jnp.int32, (1, sites), 1) % LX
    lx = lf[0]
    shifted[0] = jnp.where(xlane == 0, pltpu.roll(lx, sites - LX + 1, 1), pltpu.roll(lx, 1, 1))
    shifted[1] = pltpu.roll(lf[1], LX, 1)

    flat = lax.broadcasted_iota(jnp.int32, (1, sites), 1)
    xpos = (flat % LX).astype(jnp.float32)
    ypos = (flat // LX).astype(jnp.float32)
    width_y = sites // LX
    for k in range(ncomb):
        px = momenta_ref[k, 0].astype(jnp.float32)
        py = momenta_ref[k, 1].astype(jnp.float32)
        pz = momenta_ref[k, 2].astype(jnp.float32)
        for z in range(depth):
            zpos = (me * depth + z).astype(jnp.float32)
            angles[0, pl.ds(k * depth + z, 1), :] = 2.0 * math.pi * (
                px * xpos / LX + py * ypos / width_y + pz * zpos / total_z
            )
    theta = angles[0]
    angles[1] = jnp.cos(theta)
    angles[2] = jnp.sin(theta)

    phased[...] = jnp.zeros_like(phased)
    phased[0:nv, :] = vec_ref[0:nv, :]
    phased[128 : 128 + nv, :] = vec_ref[nv:wide, :]
    gram = lax.dot_general(
        vec_ref[...], phased[...], (((1,), (1,)), ((), ())), preferred_element_type=jnp.float32
    )
    eye = lax.broadcasted_iota(jnp.int32, (nv, 128), 0) == lax.broadcasted_iota(
        jnp.int32, (nv, 128), 1
    )
    squares = jnp.sum(
        jnp.where(eye, gram[0:nv, 0:128] + gram[nv:wide, 128:256], 0.0), axis=0, keepdims=True
    )

    disp[0] = vec_ref[...].astype(jnp.float32)

    source = lax.broadcasted_iota(jnp.int32, (sites, sites), 0)
    target = lax.broadcasted_iota(jnp.int32, (sites, sites), 1)
    row_x = target % LX
    ahead = [
        jnp.where(row_x == LX - 1, target - (LX - 1), target + 1),
        jnp.where(target >= sites - LX, target - (sites - LX), target + LX),
    ]
    behind = [
        jnp.where(row_x == 0, target + (LX - 1), target - 1),
        jnp.where(target < LX, target + (sites - LX), target - LX),
    ]

    def link_rows(ref, z, lanes):
        return [ref[pl.ds(depth * n + z, 1), lanes] for n in range(18)]

    def displaced(mu, z, forward, backward, up_links, down_links):
        for h in range(sites // 128):
            lanes = pl.ds(h * 128, 128)
            u = link_rows(up_links, z, lanes)
            w = link_rows(down_links, z, lanes)

            @pl.loop(0, nv // ROWS)
            def _(block):
                row = pl.multiple_of(block * ROWS, ROWS)
                f = [[forward(b, r, row, h) for r in range(2)] for b in range(3)]
                g = [[backward(b, r, row, h) for r in range(2)] for b in range(3)]
                for a in range(3):
                    real = 0.0
                    imag = 0.0
                    for b in range(3):
                        ur, ui = u[6 * a + 2 * b], u[6 * a + 2 * b + 1]
                        real = real + ur * f[b][0] - ui * f[b][1]
                        imag = imag + ur * f[b][1] + ui * f[b][0]
                    real_b = 0.0
                    imag_b = 0.0
                    for b in range(3):
                        wr, wi = w[6 * b + 2 * a], w[6 * b + 2 * a + 1]
                        real_b = real_b + wr * g[b][0] + wi * g[b][1]
                        imag_b = imag_b + wr * g[b][1] - wi * g[b][0]
                    at = pl.ds(z * half + a * sites + h * 128, 128)
                    disp[mu + 1, pl.ds(row, ROWS), at] = real - real_b
                    disp[mu + 1, pl.ds(row + nv, ROWS), at] = imag - imag_b

    for mu in range(2):
        plus = (source == ahead[mu]).astype(jnp.bfloat16)
        minus = (source == behind[mu]).astype(jnp.bfloat16)
        for z in range(depth):
            for c in range(3):
                cols = pl.ds(z * half + c * sites, sites)
                here = pl.ds(c * sites, sites)
                field = vec_ref[:, cols]
                moved[0, :, here] = jnp.dot(field, plus, preferred_element_type=jnp.float32)
                moved[1, :, here] = jnp.dot(field, minus, preferred_element_type=jnp.float32)

            def read(side, b, r, row, h):
                return moved[side, pl.ds(row + r * nv, ROWS), pl.ds(b * sites + h * 128, 128)]

            displaced(
                mu, z, functools.partial(read, 0), functools.partial(read, 1),
                lf.at[mu], shifted.at[mu],
            )

    for copy in halo_copies:
        copy.wait()
    for n in range(18):
        a, b, r = n // 6, (n // 2) % 3, n % 2
        shifted[0, pl.ds(depth * n, depth), :] = 0.5 * link_halo[a, b, r].astype(jnp.float32)

    def plane(index, b, r, row, h):
        rows = pl.ds(row + r * nv, ROWS)
        if index == depth:
            return halo[0, rows, pl.ds(b * sites + h * 128, 128)].astype(jnp.float32)
        if index == -1:
            return halo[1, rows, pl.ds(b * sites + h * 128, 128)].astype(jnp.float32)
        return disp[0, rows, pl.ds(index * half + b * sites + h * 128, 128)]

    for z in range(depth):
        if z > 0:
            for n in range(18):
                shifted[1, pl.ds(depth * n + z, 1), :] = lf[2, pl.ds(depth * n + z - 1, 1), :]
        else:
            for n in range(18):
                shifted[1, pl.ds(depth * n, 1), :] = shifted[0, pl.ds(depth * n + depth - 1, 1), :]
        displaced(
            2, z, functools.partial(plane, z + 1), functools.partial(plane, z - 1),
            lf.at[2], shifted.at[1],
        )

    def exchange_a(q):
        return pltpu.make_async_remote_copy(
            src_ref=send_a.at[q], dst_ref=recv_a.at[q],
            send_sem=a_send.at[q], recv_sem=a_recv.at[q],
            device_id={"space": partner}, device_id_type=MESH,
        )

    def exchange_b(q, step):
        return pltpu.make_async_remote_copy(
            src_ref=send_b.at[q, peer(step)// 2], dst_ref=recv_b.at[q, step],
            send_sem=b_send.at[q, step], recv_sem=b_recv.at[q, step],
            device_id={"space": peer(step)}, device_id_type=MESH,
        )

    lines = CHUNK * per

    def compute(k):
        q, slot = k // CHUNK, k % CHUNK
        d = directions_ref[k]
        for z in range(depth):
            cos = angles[1, pl.ds(k * depth + z, 1), :]
            sin = angles[2, pl.ds(k * depth + z, 1), :]

            @pl.loop(0, nv // ROWS)
            def _(block):
                row = pl.multiple_of(block * ROWS, ROWS)
                for c in range(3):
                    at = pl.ds(z * half + c * sites, sites)
                    real = disp[d, pl.ds(row, ROWS), at]
                    imag = disp[d, pl.ds(row + nv, ROWS), at]
                    phased[pl.ds(row, ROWS), at] = (real * cos + imag * sin).astype(jnp.bfloat16)
                    phased[pl.ds(row + 128, ROWS), at] = (imag * cos - real * sin).astype(
                        jnp.bfloat16
                    )

        full = lax.dot_general(
            vec_ref[...], phased[...], (((1,), (1,)), ((), ())), preferred_element_type=jnp.float32
        )
        raw[0] = full[0:nv, 0:128] + full[nv:wide, 128:256]
        raw[1] = full[0:nv, 128:256] - full[nv:wide, 0:128]
        for p in range(2):
            for row in range(own_rows):
                line = slot * per + p * own_rows + row
                send_a[q, line] = raw[
                    p, pl.ds(own_rows * (1 - core) + row, groups, stride=2 * own_rows), :
                ]
                total[q, line] = raw[
                    p, pl.ds(own_rows * core + row, groups, stride=2 * own_rows), :
                ]

    def forward(q):
        copy = exchange_a(q)
        copy.wait()
        for line in range(lines):
            stage[pl.ds(line, groups, stride=ROWS), :] = total[q, line] + recv_a[q, line]
        if q == 0:
            value = total[0, lines, 0:1] + recv_a[0, lines, 0:1]
            high = value.astype(jnp.bfloat16).astype(jnp.float32)
            rest = value - high
            middle = rest.astype(jnp.bfloat16).astype(jnp.float32)
            for piece, part in enumerate([high, middle, rest - middle]):
                stage[pl.ds(lines + piece, groups, stride=ROWS), :] = jnp.broadcast_to(
                    part, (groups, 128)
                )
        for g in range(groups):
            send_b[q, g] = stage[pl.ds(g * ROWS, ROWS), :].astype(jnp.bfloat16)
        own = pl.multiple_of(group * ROWS, ROWS)
        total[q, 0] = stage[pl.ds(own, ROWS), :]
        for step in range(1, groups):
            exchange_b(q, step).start()

    stage[...] = jnp.zeros_like(stage)
    send_a[0, lines] = jnp.broadcast_to(squares, (groups, 128))
    total[0, lines] = jnp.broadcast_to(squares, (groups, 128))
    for q in range(1, chunks):
        send_a[q, lines] = jnp.zeros((groups, 128), jnp.float32)
    for q in range(chunks):
        for slot in range(CHUNK):
            compute(q * CHUNK + slot)
        exchange_a(q).start()
        if q > 0:
            forward(q - 1)
    forward(chunks - 1)

    sums = []
    for q in range(chunks):
        value = total[q, 0]
        for step in range(1, groups):
            exchange_b(q, step).wait()
            value = value + recv_b[q, step].astype(jnp.float32)
        sums.append(value)
    norms = (sums[0][lines : lines + 1] + sums[0][lines + 1 : lines + 2]
             + sums[0][lines + 2 : lines + 3]) / (3.0 * volume)
    lane = lax.broadcasted_iota(jnp.int32, (1, 128), 1)
    for row in range(own_rows):
        mine = jnp.sum(
            jnp.where(lane == own_rows * me + row, norms, 0.0), axis=1, keepdims=True
        )
        scale = 1.0 / (math.sqrt(3.0 * volume) * jnp.sqrt(norms * mine))
        for k in range(ncomb):
            for p in range(2):
                line = (k % CHUNK) * per + p * own_rows + row
                value = sums[k // CHUNK][line : line + 1] * scale
                out_ref[k, row, pl.ds(p, 1), :] = value[:, 0:nv]


def elementals(vectors, links, directions, momenta):
    count = lax.axis_size("space")
    _, parts, nv, depth, sites = vectors.shape
    ncomb = directions.shape[0]
    own_rows = nv // count
    groups = count // 2
    chunks = ncomb // CHUNK
    lines = CHUNK * 2 * own_rows
    span = depth * 3 * sites
    fields = jnp.transpose(vectors, (1, 2, 3, 0, 4)).reshape(2 * nv, span)
    body = functools.partial(kernel, count, depth * count * sites, depth * count)
    smem = pl.BlockSpec(memory_space=pltpu.SMEM)
    vmem = pl.BlockSpec(memory_space=pltpu.VMEM)
    f32, bf16 = jnp.float32, jnp.bfloat16
    return pl.pallas_call(
        body,
        out_shape=jax.ShapeDtypeStruct((ncomb, own_rows, 2, nv), f32),
        in_specs=[vmem, vmem, smem, smem],
        out_specs=vmem,
        scratch_shapes=[
            pltpu.VMEM((2, 2 * nv, 3 * sites), bf16),
            pltpu.VMEM((3, 3, 2, depth, sites), bf16),
            pltpu.VMEM((3, 18 * depth, sites), f32),
            pltpu.VMEM((2, 18 * depth, sites), f32),
            pltpu.VMEM((2, 2 * nv, 3 * sites), f32),
            pltpu.VMEM((4, 2 * nv, span), f32),
            pltpu.VMEM((3, ncomb * depth, sites), f32),
            pltpu.VMEM((256, span), bf16),
            pltpu.VMEM((2, nv, 128), f32),
            pltpu.VMEM((chunks, lines + 1, groups, 128), f32),
            pltpu.VMEM((chunks, lines + 1, groups, 128), f32),
            pltpu.VMEM((groups * ROWS, 128), f32),
            pltpu.VMEM((chunks, groups, ROWS, 128), bf16),
            pltpu.VMEM((chunks, groups, ROWS, 128), bf16),
            pltpu.VMEM((chunks, lines + 1, groups, 128), f32),
            pltpu.SemaphoreType.DMA((3,)),
            pltpu.SemaphoreType.DMA((3,)),
            pltpu.SemaphoreType.DMA((chunks,)),
            pltpu.SemaphoreType.DMA((chunks,)),
            pltpu.SemaphoreType.DMA((chunks, groups)),
            pltpu.SemaphoreType.DMA((chunks, groups)),
        ],
        compiler_params=pltpu.CompilerParams(
            collective_id=0, has_side_effects=True, vmem_limit_bytes=40 * 1024 * 1024
        ),
    )(fields, links, directions, momenta)


def local(vectors, links, directions, momenta):
    slices = [
        elementals(vectors[t], links[t], directions, momenta) for t in range(vectors.shape[0])
    ]
    stacked = jnp.transpose(jnp.stack(slices), (0, 1, 3, 2, 4))
    return lax.all_gather(stacked, "tm", axis=0, tiled=True)


def solution(mesh):
    placed = (
        P("tm", None, None, None, "space", None),
        P("tm", None, None, None, None, "space", None),
        P(),
        P(),
    )
    return jax.shard_map(
        local,
        mesh=mesh,
        in_specs=placed,
        out_specs=P(None, None, None, "space", None),
        check_vma=False,
    )
```

```python
import functools
import math

import jax
import jax.numpy as jnp
from jax import lax
from jax.experimental import pallas as pl
from jax.experimental.pallas import tpu as pltpu
from jax.sharding import PartitionSpec as P

LX = 16
CHUNK = 2
ROWS = 16
BLOCK = 32
MESH = pl.DeviceIdType.MESH


def kernel(
    count, volume, total_z,
    vec_ref, links_ref, directions_ref, momenta_ref,
    out_ref,
    halo, link_halo, lf, shifted, moved, disp, angles, phased, raw, send_a, recv_a, stage, send_b, recv_b, total, final,
    halo_send, halo_recv, a_send, a_recv, b_send, b_recv,
):
    depth, _, wide, sites = vec_ref.shape
    nv = wide // 2
    half = 3 * sites
    ncomb = directions_ref.shape[0]
    own_rows = nv // count
    groups = count // 2
    per = 2 * own_rows
    chunks = ncomb // CHUNK
    me = lax.axis_index("space")
    core = lax.rem(me, 2)
    group = me // 2
    partner = me + 1 - 2 * core
    up = lax.rem(me + 1, count)
    down = lax.rem(me + count - 1, count)
    other = lax.rem(me + count - 1 + 2 * core, count)

    def peer(step):
        return lax.rem(group + step, groups) * 2 + core

    barrier = pltpu.get_barrier_semaphore()
    for target in [partner, other] + [peer(step) for step in range(1, groups)]:
        pl.semaphore_signal(barrier, inc=1, device_id={"space": target}, device_id_type=MESH)

    halo_copies = [
        pltpu.make_async_remote_copy(
            src_ref=vec_ref.at[0], dst_ref=halo.at[0],
            send_sem=halo_send.at[0], recv_sem=halo_recv.at[0],
            device_id={"space": down}, device_id_type=MESH,
        ),
        pltpu.make_async_remote_copy(
            src_ref=vec_ref.at[depth - 1], dst_ref=halo.at[1],
            send_sem=halo_send.at[1], recv_sem=halo_recv.at[1],
            device_id={"space": up}, device_id_type=MESH,
        ),
        pltpu.make_async_remote_copy(
            src_ref=links_ref.at[2], dst_ref=link_halo,
            send_sem=halo_send.at[2], recv_sem=halo_recv.at[2],
            device_id={"space": up}, device_id_type=MESH,
        ),
    ]
    along_z = [jnp.where(directions_ref[k] == 3, 1, 0) for k in range(ncomb)]
    others = ncomb - sum(along_z)
    place = []
    seen = 0
    for k in range(ncomb):
        place.append(jnp.where(along_z[k] == 1, others + seen, k - seen))
        seen = seen + along_z[k]
    order = [sum(jnp.where(place[k] == i, k, 0) for k in range(ncomb)) for i in range(ncomb)]

    for mu in range(3):
        for n in range(18):
            a, b, r = n // 6, (n // 2) % 3, n % 2
            lf[mu, pl.ds(depth * n, depth), :] = 0.5 * links_ref[mu, a, b, r].astype(jnp.float32)
    xlane = lax.broadcasted_iota(jnp.int32, (1, sites), 1) % LX
    lx = lf[0]
    shifted[0] = jnp.where(xlane == 0, pltpu.roll(lx, sites - LX + 1, 1), pltpu.roll(lx, 1, 1))
    shifted[1] = pltpu.roll(lf[1], LX, 1)

    flat = lax.broadcasted_iota(jnp.int32, (1, sites), 1)
    xpos = (flat % LX).astype(jnp.float32)
    ypos = (flat // LX).astype(jnp.float32)
    width_y = sites // LX
    for k in range(ncomb):
        px = momenta_ref[0, order[k]].astype(jnp.float32)
        py = momenta_ref[1, order[k]].astype(jnp.float32)
        pz = momenta_ref[2, order[k]].astype(jnp.float32)
        for z in range(depth):
            zpos = (me * depth + z).astype(jnp.float32)
            angles[0, pl.ds(k * depth + z, 1), :] = 2.0 * math.pi * (
                px * xpos / LX + py * ypos / width_y + pz * zpos / total_z
            )
    theta = angles[0]
    angles[1] = jnp.cos(theta)
    angles[2] = jnp.sin(theta)

    phased[...] = jnp.zeros_like(phased)
    for z in range(depth):
        for c in range(3):
            at = pl.ds(z * half + c * sites, sites)
            phased[0:nv, at] = vec_ref[z, c, 0:nv, :]
            phased[128 : 128 + nv, at] = vec_ref[z, c, nv:wide, :]
    fields = jnp.concatenate([vec_ref[z, c] for z in range(depth) for c in range(3)], axis=1)
    gram = lax.dot_general(
        fields, phased[...], (((1,), (1,)), ((), ())), preferred_element_type=jnp.float32
    )
    eye = lax.broadcasted_iota(jnp.int32, (nv, 128), 0) == lax.broadcasted_iota(
        jnp.int32, (nv, 128), 1
    )
    squares = jnp.sum(
        jnp.where(eye, gram[0:nv, 0:128] + gram[nv:wide, 128:256], 0.0), axis=0, keepdims=True
    )

    disp[0] = vec_ref[...].astype(jnp.float32)

    source = lax.broadcasted_iota(jnp.int32, (sites, sites), 0)
    target = lax.broadcasted_iota(jnp.int32, (sites, sites), 1)
    row_x = target % LX
    ahead = [
        jnp.where(row_x == LX - 1, target - (LX - 1), target + 1),
        jnp.where(target >= sites - LX, target - (sites - LX), target + LX),
    ]
    behind = [
        jnp.where(row_x == 0, target + (LX - 1), target - 1),
        jnp.where(target < LX, target + (sites - LX), target - LX),
    ]

    def link_rows(ref, z, lanes):
        return [
            jnp.broadcast_to(ref[pl.ds(depth * n + z, 1), lanes], (8, 128)) for n in range(18)
        ]

    def displaced(mu, z, forward, backward, up_links, down_links):
        for h in range(sites // 128):
            lanes = pl.ds(h * 128, 128)
            u = link_rows(up_links, z, lanes)
            w = link_rows(down_links, z, lanes)

            @pl.loop(0, nv // ROWS)
            def _(block):
                row = pl.multiple_of(block * ROWS, ROWS)

                def tiles(read, b, r):
                    return read(b, pl.ds(row + r * nv, ROWS), lanes).reshape(ROWS // 8, 8, 128)

                f = [[tiles(forward, b, r) for r in range(2)] for b in range(3)]
                g = [[tiles(backward, b, r) for r in range(2)] for b in range(3)]
                for a in range(3):
                    real = 0.0
                    imag = 0.0
                    for b in range(3):
                        ur, ui = u[6 * a + 2 * b], u[6 * a + 2 * b + 1]
                        real = real + ur * f[b][0] - ui * f[b][1]
                        imag = imag + ur * f[b][1] + ui * f[b][0]
                    real_b = 0.0
                    imag_b = 0.0
                    for b in range(3):
                        wr, wi = w[6 * b + 2 * a], w[6 * b + 2 * a + 1]
                        real_b = real_b + wr * g[b][0] + wi * g[b][1]
                        imag_b = imag_b + wr * g[b][1] - wi * g[b][0]
                    at = (mu + 1, z, a)
                    disp[(*at, pl.ds(row, ROWS), lanes)] = (real - real_b).reshape(ROWS, 128)
                    disp[(*at, pl.ds(row + nv, ROWS), lanes)] = (imag - imag_b).reshape(ROWS, 128)

    for mu in range(2):
        if mu == 1:
            pl.semaphore_wait(barrier, groups + 1)
            for copy in halo_copies:
                copy.start()
        plus = (source == ahead[mu]).astype(jnp.bfloat16)
        minus = (source == behind[mu]).astype(jnp.bfloat16)
        for z in range(depth):
            for c in range(3):
                moved[0, c] = jnp.dot(vec_ref[z, c], plus, preferred_element_type=jnp.float32)
                moved[1, c] = jnp.dot(vec_ref[z, c], minus, preferred_element_type=jnp.float32)

            def read(side, b, rows, lanes):
                return moved[side, b, rows, lanes]

            displaced(
                mu, z, functools.partial(read, 0), functools.partial(read, 1),
                lf.at[mu], shifted.at[mu],
            )

    def along_last():
        for copy in halo_copies:
            copy.wait()
        for n in range(18):
            a, b, r = n // 6, (n // 2) % 3, n % 2
            shifted[0, pl.ds(depth * n, depth), :] = 0.5 * link_halo[a, b, r].astype(jnp.float32)

        def plane(index, b, rows, lanes):
            if index == depth:
                return halo[0, b, rows, lanes].astype(jnp.float32)
            if index == -1:
                return halo[1, b, rows, lanes].astype(jnp.float32)
            return disp[0, index, b, rows, lanes]

        for z in range(depth):
            if z > 0:
                for n in range(18):
                    shifted[1, pl.ds(depth * n + z, 1), :] = lf[2, pl.ds(depth * n + z - 1, 1), :]
            else:
                for n in range(18):
                    shifted[1, pl.ds(depth * n, 1), :] = shifted[0, pl.ds(depth * n + depth - 1, 1), :]
            displaced(
                2, z, functools.partial(plane, z + 1), functools.partial(plane, z - 1),
                lf.at[2], shifted.at[1],
            )

    def exchange_a(q):
        return pltpu.make_async_remote_copy(
            src_ref=send_a.at[q], dst_ref=recv_a.at[q],
            send_sem=a_send.at[q], recv_sem=a_recv.at[q],
            device_id={"space": partner}, device_id_type=MESH,
        )

    def exchange_b(q, step):
        return pltpu.make_async_remote_copy(
            src_ref=send_b.at[q, peer(step)// 2], dst_ref=recv_b.at[q, step],
            send_sem=b_send.at[q, step], recv_sem=b_recv.at[q, step],
            device_id={"space": peer(step)}, device_id_type=MESH,
        )

    lines = CHUNK * per

    def compute(k):
        q, slot = k // CHUNK, k % CHUNK
        d = directions_ref[order[k]]
        for z in range(depth):
            cos = jnp.broadcast_to(angles[1, pl.ds(k * depth + z, 1), :], (8, sites))
            sin = jnp.broadcast_to(angles[2, pl.ds(k * depth + z, 1), :], (8, sites))

            @pl.loop(0, nv // BLOCK)
            def _(block):
                row = pl.multiple_of(block * BLOCK, BLOCK)
                for c in range(3):
                    at = pl.ds(z * half + c * sites, sites)
                    real = disp[d, z, c, pl.ds(row, BLOCK), :].reshape(BLOCK // 8, 8, sites)
                    imag = disp[d, z, c, pl.ds(row + nv, BLOCK), :].reshape(BLOCK // 8, 8, sites)
                    turned = (real * cos + imag * sin).reshape(BLOCK, sites)
                    phased[pl.ds(row, BLOCK), at] = turned.astype(jnp.bfloat16)
                    turned = (imag * cos - real * sin).reshape(BLOCK, sites)
                    phased[pl.ds(row + 128, BLOCK), at] = turned.astype(jnp.bfloat16)

        full = lax.dot_general(
            fields, phased[...], (((1,), (1,)), ((), ())), preferred_element_type=jnp.float32
        )
        raw[0] = full[0:nv, 0:128] + full[nv:wide, 128:256]
        raw[1] = full[0:nv, 128:256] - full[nv:wide, 0:128]
        for p in range(2):
            for row in range(own_rows):
                line = slot * per + p * own_rows + row
                send_a[q, line] = raw[
                    p, pl.ds(own_rows * (1 - core) + row, groups, stride=2 * own_rows), :
                ]
                total[q, line] = raw[
                    p, pl.ds(own_rows * core + row, groups, stride=2 * own_rows), :
                ]

    def forward(q):
        copy = exchange_a(q)
        copy.wait()
        for line in range(lines):
            stage[pl.ds(line, groups, stride=ROWS), :] = total[q, line] + recv_a[q, line]
        if q == 0:
            value = total[0, lines, 0:1] + recv_a[0, lines, 0:1]
            high = value.astype(jnp.bfloat16).astype(jnp.float32)
            rest = value - high
            middle = rest.astype(jnp.bfloat16).astype(jnp.float32)
            for piece, part in enumerate([high, middle, rest - middle]):
                stage[pl.ds(lines + piece, groups, stride=ROWS), :] = jnp.broadcast_to(
                    part, (groups, 128)
                )
        for g in range(groups):
            send_b[q, g] = stage[pl.ds(g * ROWS, ROWS), :].astype(jnp.bfloat16)
        own = pl.multiple_of(group * ROWS, ROWS)
        total[q, 0] = stage[pl.ds(own, ROWS), :]
        for step in range(1, groups):
            exchange_b(q, step).start()

    stage[...] = jnp.zeros_like(stage)
    send_a[0, lines] = jnp.broadcast_to(squares, (groups, 128))
    total[0, lines] = jnp.broadcast_to(squares, (groups, 128))
    for q in range(1, chunks):
        send_a[q, lines] = jnp.zeros((groups, 128), jnp.float32)
    for q in range(chunks):
        for slot in range(CHUNK):
            if q * CHUNK + slot == 3:
                along_last()
            compute(q * CHUNK + slot)
        exchange_a(q).start()
        if q > 0:
            forward(q - 1)
    forward(chunks - 1)

    sums = []
    for q in range(chunks):
        value = total[q, 0]
        for step in range(1, groups):
            exchange_b(q, step).wait()
            value = value + recv_b[q, step].astype(jnp.float32)
        sums.append(value)
        for slot in range(CHUNK):
            final[q * CHUNK + slot, pl.ds(0, per), :] = value[slot * per : (slot + 1) * per]
    norms = (sums[0][lines : lines + 1] + sums[0][lines + 1 : lines + 2]
             + sums[0][lines + 2 : lines + 3]) / (3.0 * volume)
    lane = lax.broadcasted_iota(jnp.int32, (1, 128), 1)
    for row in range(own_rows):
        mine = jnp.sum(
            jnp.where(lane == own_rows * me + row, norms, 0.0), axis=1, keepdims=True
        )
        scale = 1.0 / (math.sqrt(3.0 * volume) * jnp.sqrt(norms * mine))
        for k in range(ncomb):
            for p in range(2):
                value = final[place[k], pl.ds(p * own_rows + row, 1), :] * scale
                out_ref[k, row, pl.ds(p, 1), :] = value[:, 0:nv]


def elementals(vectors, links, directions, momenta):
    count = lax.axis_size("space")
    _, parts, nv, depth, sites = vectors.shape
    ncomb = directions.shape[0]
    own_rows = nv // count
    groups = count // 2
    chunks = ncomb // CHUNK
    lines = CHUNK * 2 * own_rows
    span = depth * 3 * sites
    fields = jnp.transpose(vectors, (3, 0, 1, 2, 4)).reshape(depth, 3, 2 * nv, sites)
    body = functools.partial(kernel, count, depth * count * sites, depth * count)
    smem = pl.BlockSpec(memory_space=pltpu.SMEM)
    vmem = pl.BlockSpec(memory_space=pltpu.VMEM)
    f32, bf16 = jnp.float32, jnp.bfloat16
    return pl.pallas_call(
        body,
        out_shape=jax.ShapeDtypeStruct((ncomb, own_rows, 2, nv), f32),
        in_specs=[vmem, vmem, smem, smem],
        out_specs=vmem,
        scratch_shapes=[
            pltpu.VMEM((2, 3, 2 * nv, sites), bf16),
            pltpu.VMEM((3, 3, 2, depth, sites), bf16),
            pltpu.VMEM((3, 18 * depth, sites), f32),
            pltpu.VMEM((2, 18 * depth, sites), f32),
            pltpu.VMEM((2, 3, 2 * nv, sites), f32),
            pltpu.VMEM((4, depth, 3, 2 * nv, sites), f32),
            pltpu.VMEM((3, ncomb * depth, sites), f32),
            pltpu.VMEM((256, span), bf16),
            pltpu.VMEM((2, nv, 128), f32),
            pltpu.VMEM((chunks, lines + 1, groups, 128), f32),
            pltpu.VMEM((chunks, lines + 1, groups, 128), f32),
            pltpu.VMEM((groups * ROWS, 128), f32),
            pltpu.VMEM((chunks, groups, ROWS, 128), bf16),
            pltpu.VMEM((chunks, groups, ROWS, 128), bf16),
            pltpu.VMEM((chunks, lines + 1, groups, 128), f32),
            pltpu.VMEM((ncomb, 8, 128), f32),
            pltpu.SemaphoreType.DMA((3,)),
            pltpu.SemaphoreType.DMA((3,)),
            pltpu.SemaphoreType.DMA((chunks,)),
            pltpu.SemaphoreType.DMA((chunks,)),
            pltpu.SemaphoreType.DMA((chunks, groups)),
            pltpu.SemaphoreType.DMA((chunks, groups)),
        ],
        compiler_params=pltpu.CompilerParams(
            collective_id=0, has_side_effects=True, vmem_limit_bytes=40 * 1024 * 1024
        ),
    )(fields, links, directions, jnp.transpose(momenta))


def local(vectors, links, directions, momenta):
    slices = [
        elementals(vectors[t], links[t], directions, momenta) for t in range(vectors.shape[0])
    ]
    stacked = jnp.transpose(jnp.stack(slices), (0, 1, 3, 2, 4))
    return lax.all_gather(stacked, "tm", axis=0, tiled=True)


def solution(mesh):
    placed = (
        P("tm", None, None, None, "space", None),
        P("tm", None, None, None, None, "space", None),
        P(),
        P(),
    )
    return jax.shard_map(
        local,
        mesh=mesh,
        in_specs=placed,
        out_specs=P(None, None, None, "space", None),
        check_vma=False,
    )
```

```python
import functools
import math

import jax
import jax.numpy as jnp
from jax import lax
from jax.experimental import pallas as pl
from jax.experimental.pallas import tpu as pltpu
from jax.sharding import PartitionSpec as P

LX = 16
SIZES = (3, 2, 1)
ROWS = 32
BLOCK = 32
MESH = pl.DeviceIdType.MESH


def kernel(
    count, volume, total_z,
    vec_ref, links_ref, directions_ref, momenta_ref,
    out_ref,
    halo, link_halo, lf, shifted, moved, disp, angles, phased, raw, send_a, recv_a, stage, *rest,
):
    send_b, recv_b = rest[: len(SIZES)], rest[len(SIZES) : 2 * len(SIZES)]
    own, total, final, halo_send, halo_recv, a_send, a_recv, b_send, b_recv = rest[2 * len(SIZES) :]
    depth, _, wide, sites = vec_ref.shape
    nv = wide // 2
    half = 3 * sites
    ncomb = directions_ref.shape[0]
    own_rows = nv // count
    groups = count // 2
    per = 2 * own_rows
    chunks = len(SIZES)
    starts = [sum(SIZES[:q]) for q in range(chunks)]
    lines = [size * per for size in SIZES]
    heights = [buffer.shape[1] for buffer in send_b]
    me = lax.axis_index("space")
    core = lax.rem(me, 2)
    group = me // 2
    partner = me + 1 - 2 * core
    up = lax.rem(me + 1, count)
    down = lax.rem(me + count - 1, count)
    other = lax.rem(me + count - 1 + 2 * core, count)

    def peer(step):
        return lax.rem(group + step, groups) * 2 + core

    barrier = pltpu.get_barrier_semaphore()
    for target in [partner, other] + [peer(step) for step in range(1, groups)]:
        pl.semaphore_signal(barrier, inc=1, device_id={"space": target}, device_id_type=MESH)

    halo_copies = [
        pltpu.make_async_remote_copy(
            src_ref=vec_ref.at[0], dst_ref=halo.at[0],
            send_sem=halo_send.at[0], recv_sem=halo_recv.at[0],
            device_id={"space": down}, device_id_type=MESH,
        ),
        pltpu.make_async_remote_copy(
            src_ref=vec_ref.at[depth - 1], dst_ref=halo.at[1],
            send_sem=halo_send.at[1], recv_sem=halo_recv.at[1],
            device_id={"space": up}, device_id_type=MESH,
        ),
        pltpu.make_async_remote_copy(
            src_ref=links_ref.at[2], dst_ref=link_halo,
            send_sem=halo_send.at[2], recv_sem=halo_recv.at[2],
            device_id={"space": up}, device_id_type=MESH,
        ),
    ]
    along_z = [jnp.where(directions_ref[k] == 3, 1, 0) for k in range(ncomb)]
    others = ncomb - sum(along_z)
    place = []
    seen = 0
    for k in range(ncomb):
        place.append(jnp.where(along_z[k] == 1, others + seen, k - seen))
        seen = seen + along_z[k]
    order = [sum(jnp.where(place[k] == i, k, 0) for k in range(ncomb)) for i in range(ncomb)]

    for mu in range(3):
        for n in range(18):
            a, b, r = n // 6, (n // 2) % 3, n % 2
            lf[mu, pl.ds(depth * n, depth), :] = 0.5 * links_ref[mu, a, b, r].astype(jnp.float32)
    xlane = lax.broadcasted_iota(jnp.int32, (1, sites), 1) % LX
    lx = lf[0]
    shifted[0] = jnp.where(xlane == 0, pltpu.roll(lx, sites - LX + 1, 1), pltpu.roll(lx, 1, 1))
    shifted[1] = pltpu.roll(lf[1], LX, 1)

    flat = lax.broadcasted_iota(jnp.int32, (1, sites), 1)
    xpos = (flat % LX).astype(jnp.float32)
    ypos = (flat // LX).astype(jnp.float32)
    width_y = sites // LX
    for k in range(ncomb):
        px = momenta_ref[0, order[k]].astype(jnp.float32)
        py = momenta_ref[1, order[k]].astype(jnp.float32)
        pz = momenta_ref[2, order[k]].astype(jnp.float32)
        for z in range(depth):
            zpos = (me * depth + z).astype(jnp.float32)
            angles[0, pl.ds(k * depth + z, 1), :] = 2.0 * math.pi * (
                px * xpos / LX + py * ypos / width_y + pz * zpos / total_z
            )
    theta = angles[0]
    angles[1] = jnp.cos(theta)
    angles[2] = jnp.sin(theta)

    phased[...] = jnp.zeros_like(phased)
    for z in range(depth):
        for c in range(3):
            at = pl.ds(z * half + c * sites, sites)
            phased[0:nv, at] = vec_ref[z, c, 0:nv, :]
            phased[128 : 128 + nv, at] = vec_ref[z, c, nv:wide, :]
    fields = jnp.concatenate([vec_ref[z, c] for z in range(depth) for c in range(3)], axis=1)
    gram = lax.dot_general(
        fields, phased[...], (((1,), (1,)), ((), ())), preferred_element_type=jnp.float32
    )
    eye = lax.broadcasted_iota(jnp.int32, (nv, 128), 0) == lax.broadcasted_iota(
        jnp.int32, (nv, 128), 1
    )
    squares = jnp.sum(
        jnp.where(eye, gram[0:nv, 0:128] + gram[nv:wide, 128:256], 0.0), axis=0, keepdims=True
    )

    disp[0] = vec_ref[...].astype(jnp.float32)

    source = lax.broadcasted_iota(jnp.int32, (sites, sites), 0)
    target = lax.broadcasted_iota(jnp.int32, (sites, sites), 1)
    row_x = target % LX
    ahead = [
        jnp.where(row_x == LX - 1, target - (LX - 1), target + 1),
        jnp.where(target >= sites - LX, target - (sites - LX), target + LX),
    ]
    behind = [
        jnp.where(row_x == 0, target + (LX - 1), target - 1),
        jnp.where(target < LX, target + (sites - LX), target - LX),
    ]

    def link_rows(ref, z, lanes):
        return [
            jnp.broadcast_to(ref[pl.ds(depth * n + z, 1), lanes], (8, 128)) for n in range(18)
        ]

    def displaced(mu, z, forward, backward, up_links, down_links):
        for h in range(sites // 128):
            lanes = pl.ds(h * 128, 128)
            u = link_rows(up_links, z, lanes)
            w = link_rows(down_links, z, lanes)

            @pl.loop(0, nv // ROWS)
            def _(block):
                row = pl.multiple_of(block * ROWS, ROWS)

                def tiles(read, b, r):
                    return read(b, pl.ds(row + r * nv, ROWS), lanes).reshape(ROWS // 8, 8, 128)

                f = [[tiles(forward, b, r) for r in range(2)] for b in range(3)]
                g = [[tiles(backward, b, r) for r in range(2)] for b in range(3)]
                for a in range(3):
                    real = 0.0
                    imag = 0.0
                    for b in range(3):
                        ur, ui = u[6 * a + 2 * b], u[6 * a + 2 * b + 1]
                        real = real + ur * f[b][0] - ui * f[b][1]
                        imag = imag + ur * f[b][1] + ui * f[b][0]
                    real_b = 0.0
                    imag_b = 0.0
                    for b in range(3):
                        wr, wi = w[6 * b + 2 * a], w[6 * b + 2 * a + 1]
                        real_b = real_b + wr * g[b][0] + wi * g[b][1]
                        imag_b = imag_b + wr * g[b][1] - wi * g[b][0]
                    at = (mu + 1, z, a)
                    disp[(*at, pl.ds(row, ROWS), lanes)] = (real - real_b).reshape(ROWS, 128)
                    disp[(*at, pl.ds(row + nv, ROWS), lanes)] = (imag - imag_b).reshape(ROWS, 128)

    for mu in range(2):
        if mu == 0:
            pl.semaphore_wait(barrier, groups + 1)
            for copy in halo_copies:
                copy.start()
        plus = (source == ahead[mu]).astype(jnp.bfloat16)
        minus = (source == behind[mu]).astype(jnp.bfloat16)
        for z in range(depth):
            for c in range(3):
                moved[0, c] = jnp.dot(vec_ref[z, c], plus, preferred_element_type=jnp.float32)
                moved[1, c] = jnp.dot(vec_ref[z, c], minus, preferred_element_type=jnp.float32)

            def read(side, b, rows, lanes):
                return moved[side, b, rows, lanes]

            displaced(
                mu, z, functools.partial(read, 0), functools.partial(read, 1),
                lf.at[mu], shifted.at[mu],
            )

    def along_last():
        for copy in halo_copies:
            copy.wait()
        for n in range(18):
            a, b, r = n // 6, (n // 2) % 3, n % 2
            shifted[0, pl.ds(depth * n, depth), :] = 0.5 * link_halo[a, b, r].astype(jnp.float32)

        def plane(index, b, rows, lanes):
            if index == depth:
                return halo[0, b, rows, lanes].astype(jnp.float32)
            if index == -1:
                return halo[1, b, rows, lanes].astype(jnp.float32)
            return disp[0, index, b, rows, lanes]

        for z in range(depth):
            if z > 0:
                for n in range(18):
                    shifted[1, pl.ds(depth * n + z, 1), :] = lf[2, pl.ds(depth * n + z - 1, 1), :]
            else:
                for n in range(18):
                    shifted[1, pl.ds(depth * n, 1), :] = shifted[0, pl.ds(depth * n + depth - 1, 1), :]
            displaced(
                2, z, functools.partial(plane, z + 1), functools.partial(plane, z - 1),
                lf.at[2], shifted.at[1],
            )

    def exchange_a(q):
        return pltpu.make_async_remote_copy(
            src_ref=send_a.at[q, pl.ds(0, lines[q] + (q == 0))],
            dst_ref=recv_a.at[q, pl.ds(0, lines[q] + (q == 0))],
            send_sem=a_send.at[q], recv_sem=a_recv.at[q],
            device_id={"space": partner}, device_id_type=MESH,
        )

    def exchange_b(q, step):
        return pltpu.make_async_remote_copy(
            src_ref=send_b[q].at[peer(step) // 2], dst_ref=recv_b[q].at[step],
            send_sem=b_send.at[q, step], recv_sem=b_recv.at[q, step],
            device_id={"space": peer(step)}, device_id_type=MESH,
        )

    def compute(q, slot):
        k = starts[q] + slot
        d = directions_ref[order[k]]
        for z in range(depth):
            cos = jnp.broadcast_to(angles[1, pl.ds(k * depth + z, 1), :], (8, sites))
            sin = jnp.broadcast_to(angles[2, pl.ds(k * depth + z, 1), :], (8, sites))

            @pl.loop(0, nv // BLOCK)
            def _(block):
                row = pl.multiple_of(block * BLOCK, BLOCK)
                for c in range(3):
                    at = pl.ds(z * half + c * sites, sites)
                    real = disp[d, z, c, pl.ds(row, BLOCK), :].reshape(BLOCK // 8, 8, sites)
                    imag = disp[d, z, c, pl.ds(row + nv, BLOCK), :].reshape(BLOCK // 8, 8, sites)
                    turned = (real * cos + imag * sin).reshape(BLOCK, sites)
                    phased[pl.ds(row, BLOCK), at] = turned.astype(jnp.bfloat16)
                    turned = (imag * cos - real * sin).reshape(BLOCK, sites)
                    phased[pl.ds(row + 128, BLOCK), at] = turned.astype(jnp.bfloat16)

        full = lax.dot_general(
            fields, phased[...], (((1,), (1,)), ((), ())), preferred_element_type=jnp.float32
        )
        raw[0] = full[0:nv, 0:128] + full[nv:wide, 128:256]
        raw[1] = full[0:nv, 128:256] - full[nv:wide, 0:128]
        for p in range(2):
            for row in range(own_rows):
                line = slot * per + p * own_rows + row
                send_a[q, line] = raw[
                    p, pl.ds(own_rows * (1 - core) + row, groups, stride=2 * own_rows), :
                ]
                total[q, line] = raw[
                    p, pl.ds(own_rows * core + row, groups, stride=2 * own_rows), :
                ]

    def forward(q):
        copy = exchange_a(q)
        copy.wait()
        height = heights[q]
        for line in range(lines[q]):
            stage[pl.ds(line, groups, stride=height), :] = total[q, line] + recv_a[q, line]
        if q == 0:
            value = total[0, lines[0], 0:1] + recv_a[0, lines[0], 0:1]
            high = value.astype(jnp.bfloat16).astype(jnp.float32)
            low = value - high
            middle = low.astype(jnp.bfloat16).astype(jnp.float32)
            for piece, part in enumerate([high, middle, low - middle]):
                stage[pl.ds(lines[0] + piece, groups, stride=height), :] = jnp.broadcast_to(
                    part, (groups, 128)
                )
        for g in range(groups):
            send_b[q][g] = stage[pl.ds(g * height, height), :].astype(jnp.bfloat16)
        for step in range(1, groups):
            exchange_b(q, step).start()
        at = pl.multiple_of(group * height, 8)
        own[q, pl.ds(0, height), :] = stage[pl.ds(at, height), :]

    stage[...] = jnp.zeros_like(stage)
    send_a[0, lines[0]] = jnp.broadcast_to(squares, (groups, 128))
    total[0, lines[0]] = jnp.broadcast_to(squares, (groups, 128))
    for q in range(chunks):
        if q == 1:
            along_last()
            forward(0)
        for slot in range(SIZES[q]):
            compute(q, slot)
        exchange_a(q).start()
        if q > 1:
            forward(q - 1)
    forward(chunks - 1)

    sums = []
    for q in range(chunks):
        value = own[q, pl.ds(0, heights[q]), :]
        for step in range(1, groups):
            exchange_b(q, step).wait()
            value = value + recv_b[q][step].astype(jnp.float32)
        sums.append(value)
        for slot in range(SIZES[q]):
            final[starts[q] + slot, pl.ds(0, per), :] = value[slot * per : (slot + 1) * per]
    first = lines[0]
    norms = (
        sums[0][first : first + 1] + sums[0][first + 1 : first + 2] + sums[0][first + 2 : first + 3]
    ) / (3.0 * volume)
    lane = lax.broadcasted_iota(jnp.int32, (1, 128), 1)
    for row in range(own_rows):
        mine = jnp.sum(
            jnp.where(lane == own_rows * me + row, norms, 0.0), axis=1, keepdims=True
        )
        scale = 1.0 / (math.sqrt(3.0 * volume) * jnp.sqrt(norms * mine))
        for k in range(ncomb):
            for p in range(2):
                value = final[place[k], pl.ds(p * own_rows + row, 1), :] * scale
                out_ref[k, row, pl.ds(p, 1), :] = value[:, 0:nv]


def elementals(vectors, links, directions, momenta):
    count = lax.axis_size("space")
    _, parts, nv, depth, sites = vectors.shape
    ncomb = directions.shape[0]
    own_rows = nv // count
    groups = count // 2
    chunks = len(SIZES)
    lines = [size * 2 * own_rows + (q == 0) for q, size in enumerate(SIZES)]
    heights = [-(-(n + 2 * (q == 0)) // 8) * 8 for q, n in enumerate(lines)]
    height = max(heights)
    span = depth * 3 * sites
    fields = jnp.transpose(vectors, (3, 0, 1, 2, 4)).reshape(depth, 3, 2 * nv, sites)
    body = functools.partial(kernel, count, depth * count * sites, depth * count)
    smem = pl.BlockSpec(memory_space=pltpu.SMEM)
    vmem = pl.BlockSpec(memory_space=pltpu.VMEM)
    f32, bf16 = jnp.float32, jnp.bfloat16
    return pl.pallas_call(
        body,
        out_shape=jax.ShapeDtypeStruct((ncomb, own_rows, 2, nv), f32),
        in_specs=[vmem, vmem, smem, smem],
        out_specs=vmem,
        scratch_shapes=[
            pltpu.VMEM((2, 3, 2 * nv, sites), bf16),
            pltpu.VMEM((3, 3, 2, depth, sites), bf16),
            pltpu.VMEM((3, 18 * depth, sites), f32),
            pltpu.VMEM((2, 18 * depth, sites), f32),
            pltpu.VMEM((2, 3, 2 * nv, sites), f32),
            pltpu.VMEM((4, depth, 3, 2 * nv, sites), f32),
            pltpu.VMEM((3, ncomb * depth, sites), f32),
            pltpu.VMEM((256, span), bf16),
            pltpu.VMEM((2, nv, 128), f32),
            pltpu.VMEM((chunks, max(lines), groups, 128), f32),
            pltpu.VMEM((chunks, max(lines), groups, 128), f32),
            pltpu.VMEM((groups * height, 128), f32),
            *[pltpu.VMEM((groups, rows, 128), bf16) for rows in heights],
            *[pltpu.VMEM((groups, rows, 128), bf16) for rows in heights],
            pltpu.VMEM((chunks, height, 128), f32),
            pltpu.VMEM((chunks, max(lines), groups, 128), f32),
            pltpu.VMEM((ncomb, 8, 128), f32),
            pltpu.SemaphoreType.DMA((3,)),
            pltpu.SemaphoreType.DMA((3,)),
            pltpu.SemaphoreType.DMA((chunks,)),
            pltpu.SemaphoreType.DMA((chunks,)),
            pltpu.SemaphoreType.DMA((chunks, groups)),
            pltpu.SemaphoreType.DMA((chunks, groups)),
        ],
        compiler_params=pltpu.CompilerParams(
            collective_id=0, has_side_effects=True, vmem_limit_bytes=40 * 1024 * 1024
        ),
    )(fields, links, directions, jnp.transpose(momenta))


def local(vectors, links, directions, momenta):
    slices = [
        elementals(vectors[t], links[t], directions, momenta) for t in range(vectors.shape[0])
    ]
    stacked = jnp.transpose(jnp.stack(slices), (0, 1, 3, 2, 4))
    return lax.all_gather(stacked, "tm", axis=0, tiled=True)


def solution(mesh):
    placed = (
        P("tm", None, None, None, "space", None),
        P("tm", None, None, None, None, "space", None),
        P(),
        P(),
    )
    return jax.shard_map(
        local,
        mesh=mesh,
        in_specs=placed,
        out_specs=P(None, None, None, "space", None),
        check_vma=False,
    )
```

```python
import functools
import math

import jax
import jax.numpy as jnp
from jax import lax
from jax.experimental import pallas as pl
from jax.experimental.pallas import tpu as pltpu
from jax.sharding import PartitionSpec as P

LX = 16
SIZES = (3, 2, 1)
ROWS = 48
BLOCK = 96
MESH = pl.DeviceIdType.MESH


def kernel(
    count, volume, total_z,
    vec_ref, links_ref, directions_ref, momenta_ref,
    out_ref,
    halo, link_halo, lf, shifted, moved, disp, angles, phased, raw, send_a, recv_a, stage, *rest,
):
    send_b, recv_b = rest[: len(SIZES)], rest[len(SIZES) : 2 * len(SIZES)]
    own, total, final, halo_send, halo_recv, a_send, a_recv, b_send, b_recv = rest[2 * len(SIZES) :]
    depth, _, wide, sites = vec_ref.shape
    nv = wide // 2
    half = 3 * sites
    ncomb = directions_ref.shape[0]
    own_rows = nv // count
    groups = count // 2
    per = 2 * own_rows
    chunks = len(SIZES)
    starts = [sum(SIZES[:q]) for q in range(chunks)]
    lines = [size * per for size in SIZES]
    heights = [buffer.shape[1] for buffer in send_b]
    me = lax.axis_index("space")
    core = lax.rem(me, 2)
    group = me // 2
    partner = me + 1 - 2 * core
    up = lax.rem(me + 1, count)
    down = lax.rem(me + count - 1, count)
    other = lax.rem(me + count - 1 + 2 * core, count)

    def peer(step):
        return lax.rem(group + step, groups) * 2 + core

    barrier = pltpu.get_barrier_semaphore()
    for target in [partner, other] + [peer(step) for step in range(1, groups)]:
        pl.semaphore_signal(barrier, inc=1, device_id={"space": target}, device_id_type=MESH)

    halo_copies = [
        pltpu.make_async_remote_copy(
            src_ref=vec_ref.at[0], dst_ref=halo.at[0],
            send_sem=halo_send.at[0], recv_sem=halo_recv.at[0],
            device_id={"space": down}, device_id_type=MESH,
        ),
        pltpu.make_async_remote_copy(
            src_ref=vec_ref.at[depth - 1], dst_ref=halo.at[1],
            send_sem=halo_send.at[1], recv_sem=halo_recv.at[1],
            device_id={"space": up}, device_id_type=MESH,
        ),
        pltpu.make_async_remote_copy(
            src_ref=links_ref.at[2], dst_ref=link_halo,
            send_sem=halo_send.at[2], recv_sem=halo_recv.at[2],
            device_id={"space": up}, device_id_type=MESH,
        ),
    ]
    along_z = [jnp.where(directions_ref[k] == 3, 1, 0) for k in range(ncomb)]
    others = ncomb - sum(along_z)
    place = []
    seen = 0
    for k in range(ncomb):
        place.append(jnp.where(along_z[k] == 1, others + seen, k - seen))
        seen = seen + along_z[k]
    order = [sum(jnp.where(place[k] == i, k, 0) for k in range(ncomb)) for i in range(ncomb)]

    for mu in range(3):
        for n in range(18):
            a, b, r = n // 6, (n // 2) % 3, n % 2
            lf[mu, pl.ds(depth * n, depth), :] = 0.5 * links_ref[mu, a, b, r].astype(jnp.float32)
    xlane = lax.broadcasted_iota(jnp.int32, (1, sites), 1) % LX
    lx = lf[0]
    shifted[0] = jnp.where(xlane == 0, pltpu.roll(lx, sites - LX + 1, 1), pltpu.roll(lx, 1, 1))
    shifted[1] = pltpu.roll(lf[1], LX, 1)

    flat = lax.broadcasted_iota(jnp.int32, (1, sites), 1)
    xpos = (flat % LX).astype(jnp.float32)
    ypos = (flat // LX).astype(jnp.float32)
    width_y = sites // LX
    for k in range(ncomb):
        px = momenta_ref[0, order[k]].astype(jnp.float32)
        py = momenta_ref[1, order[k]].astype(jnp.float32)
        pz = momenta_ref[2, order[k]].astype(jnp.float32)
        for z in range(depth):
            zpos = (me * depth + z).astype(jnp.float32)
            angles[0, pl.ds(k * depth + z, 1), :] = 2.0 * math.pi * (
                px * xpos / LX + py * ypos / width_y + pz * zpos / total_z
            )
    theta = angles[0]
    angles[1] = jnp.cos(theta)
    angles[2] = jnp.sin(theta)

    phased[...] = jnp.zeros_like(phased)
    for z in range(depth):
        for c in range(3):
            at = pl.ds(z * half + c * sites, sites)
            phased[0:nv, at] = vec_ref[z, c, 0:nv, :]
            phased[128 : 128 + nv, at] = vec_ref[z, c, nv:wide, :]
    fields = jnp.concatenate([vec_ref[z, c] for z in range(depth) for c in range(3)], axis=1)
    gram = lax.dot_general(
        fields, phased[...], (((1,), (1,)), ((), ())), preferred_element_type=jnp.float32
    )
    eye = lax.broadcasted_iota(jnp.int32, (nv, 128), 0) == lax.broadcasted_iota(
        jnp.int32, (nv, 128), 1
    )
    squares = jnp.sum(
        jnp.where(eye, gram[0:nv, 0:128] + gram[nv:wide, 128:256], 0.0), axis=0, keepdims=True
    )

    disp[0] = vec_ref[...].astype(jnp.float32)

    source = lax.broadcasted_iota(jnp.int32, (sites, sites), 0)
    target = lax.broadcasted_iota(jnp.int32, (sites, sites), 1)
    row_x = target % LX
    ahead = [
        jnp.where(row_x == LX - 1, target - (LX - 1), target + 1),
        jnp.where(target >= sites - LX, target - (sites - LX), target + LX),
    ]
    behind = [
        jnp.where(row_x == 0, target + (LX - 1), target - 1),
        jnp.where(target < LX, target + (sites - LX), target - LX),
    ]

    def link_rows(ref, z, lanes):
        return [
            jnp.broadcast_to(ref[pl.ds(depth * n + z, 1), lanes], (8, 128)) for n in range(18)
        ]

    def displaced(mu, z, forward, backward, up_links, down_links):
        for h in range(sites // 128):
            lanes = pl.ds(h * 128, 128)
            u = link_rows(up_links, z, lanes)
            w = link_rows(down_links, z, lanes)

            @pl.loop(0, nv // ROWS)
            def _(block):
                row = pl.multiple_of(block * ROWS, ROWS)

                def tiles(read, b, r):
                    return read(b, pl.ds(row + r * nv, ROWS), lanes).reshape(ROWS // 8, 8, 128)

                f = [[tiles(forward, b, r) for r in range(2)] for b in range(3)]
                g = [[tiles(backward, b, r) for r in range(2)] for b in range(3)]
                for a in range(3):
                    real = 0.0
                    imag = 0.0
                    for b in range(3):
                        ur, ui = u[6 * a + 2 * b], u[6 * a + 2 * b + 1]
                        real = real + ur * f[b][0] - ui * f[b][1]
                        imag = imag + ur * f[b][1] + ui * f[b][0]
                    real_b = 0.0
                    imag_b = 0.0
                    for b in range(3):
                        wr, wi = w[6 * b + 2 * a], w[6 * b + 2 * a + 1]
                        real_b = real_b + wr * g[b][0] + wi * g[b][1]
                        imag_b = imag_b + wr * g[b][1] - wi * g[b][0]
                    at = (mu + 1, z, a)
                    disp[(*at, pl.ds(row, ROWS), lanes)] = (real - real_b).reshape(ROWS, 128)
                    disp[(*at, pl.ds(row + nv, ROWS), lanes)] = (imag - imag_b).reshape(ROWS, 128)

    for mu in range(2):
        if mu == 0:
            pl.semaphore_wait(barrier, groups + 1)
            for copy in halo_copies:
                copy.start()
        plus = (source == ahead[mu]).astype(jnp.bfloat16)
        minus = (source == behind[mu]).astype(jnp.bfloat16)
        for z in range(depth):
            for c in range(3):
                moved[0, c] = jnp.dot(vec_ref[z, c], plus, preferred_element_type=jnp.float32)
                moved[1, c] = jnp.dot(vec_ref[z, c], minus, preferred_element_type=jnp.float32)

            def read(side, b, rows, lanes):
                return moved[side, b, rows, lanes]

            displaced(
                mu, z, functools.partial(read, 0), functools.partial(read, 1),
                lf.at[mu], shifted.at[mu],
            )

    def along_last():
        for copy in halo_copies:
            copy.wait()
        for n in range(18):
            a, b, r = n // 6, (n // 2) % 3, n % 2
            shifted[0, pl.ds(depth * n, depth), :] = 0.5 * link_halo[a, b, r].astype(jnp.float32)

        def plane(index, b, rows, lanes):
            if index == depth:
                return halo[0, b, rows, lanes].astype(jnp.float32)
            if index == -1:
                return halo[1, b, rows, lanes].astype(jnp.float32)
            return disp[0, index, b, rows, lanes]

        for z in range(depth):
            if z > 0:
                for n in range(18):
                    shifted[1, pl.ds(depth * n + z, 1), :] = lf[2, pl.ds(depth * n + z - 1, 1), :]
            else:
                for n in range(18):
                    shifted[1, pl.ds(depth * n, 1), :] = shifted[0, pl.ds(depth * n + depth - 1, 1), :]
            displaced(
                2, z, functools.partial(plane, z + 1), functools.partial(plane, z - 1),
                lf.at[2], shifted.at[1],
            )

    def exchange_a(q):
        return pltpu.make_async_remote_copy(
            src_ref=send_a.at[q, pl.ds(0, lines[q] + (q == 0))],
            dst_ref=recv_a.at[q, pl.ds(0, lines[q] + (q == 0))],
            send_sem=a_send.at[q], recv_sem=a_recv.at[q],
            device_id={"space": partner}, device_id_type=MESH,
        )

    def exchange_b(q, step):
        return pltpu.make_async_remote_copy(
            src_ref=send_b[q].at[peer(step) // 2], dst_ref=recv_b[q].at[step],
            send_sem=b_send.at[q], recv_sem=b_recv.at[q],
            device_id={"space": peer(step)}, device_id_type=MESH,
        )

    def compute(q, slot):
        k = starts[q] + slot
        d = directions_ref[order[k]]
        for z in range(depth):
            cos = jnp.broadcast_to(angles[1, pl.ds(k * depth + z, 1), :], (8, sites))
            sin = jnp.broadcast_to(angles[2, pl.ds(k * depth + z, 1), :], (8, sites))

            @pl.loop(0, nv // BLOCK)
            def _(block):
                row = pl.multiple_of(block * BLOCK, BLOCK)
                for c in range(3):
                    at = pl.ds(z * half + c * sites, sites)
                    real = disp[d, z, c, pl.ds(row, BLOCK), :].reshape(BLOCK // 8, 8, sites)
                    imag = disp[d, z, c, pl.ds(row + nv, BLOCK), :].reshape(BLOCK // 8, 8, sites)
                    turned = (real * cos + imag * sin).reshape(BLOCK, sites)
                    phased[pl.ds(row, BLOCK), at] = turned.astype(jnp.bfloat16)
                    turned = (imag * cos - real * sin).reshape(BLOCK, sites)
                    phased[pl.ds(row + 128, BLOCK), at] = turned.astype(jnp.bfloat16)

        full = lax.dot_general(
            fields, phased[...], (((1,), (1,)), ((), ())), preferred_element_type=jnp.float32
        )
        raw[0] = full[0:nv, 0:128] + full[nv:wide, 128:256]
        raw[1] = full[0:nv, 128:256] - full[nv:wide, 0:128]
        for p in range(2):
            for row in range(own_rows):
                line = slot * per + p * own_rows + row
                send_a[q, line] = raw[
                    p, pl.ds(own_rows * (1 - core) + row, groups, stride=2 * own_rows), :
                ]
                total[q, line] = raw[
                    p, pl.ds(own_rows * core + row, groups, stride=2 * own_rows), :
                ]

    def forward(q):
        copy = exchange_a(q)
        copy.wait()
        height = heights[q]
        for line in range(lines[q]):
            stage[pl.ds(line, groups, stride=height), :] = total[q, line] + recv_a[q, line]
        if q == 0:
            value = total[0, lines[0], 0:1] + recv_a[0, lines[0], 0:1]
            high = value.astype(jnp.bfloat16).astype(jnp.float32)
            low = value - high
            middle = low.astype(jnp.bfloat16).astype(jnp.float32)
            for piece, part in enumerate([high, middle, low - middle]):
                stage[pl.ds(lines[0] + piece, groups, stride=height), :] = jnp.broadcast_to(
                    part, (groups, 128)
                )
        for g in range(groups):
            send_b[q][g] = stage[pl.ds(g * height, height), :].astype(jnp.bfloat16)
        for step in range(1, groups):
            exchange_b(q, step).start()
        at = pl.multiple_of(group * height, 8)
        own[q, pl.ds(0, height), :] = stage[pl.ds(at, height), :]

    stage[...] = jnp.zeros_like(stage)
    send_a[0, lines[0]] = jnp.broadcast_to(squares, (groups, 128))
    total[0, lines[0]] = jnp.broadcast_to(squares, (groups, 128))
    for q in range(chunks):
        if q == 1:
            along_last()
            forward(0)
        for slot in range(SIZES[q]):
            compute(q, slot)
        exchange_a(q).start()
        if q > 1:
            forward(q - 1)
    forward(chunks - 1)

    sums = []
    for q in range(chunks):
        pltpu.make_async_remote_copy(
            src_ref=send_b[q].at[pl.ds(0, groups - 1)], dst_ref=recv_b[q].at[pl.ds(1, groups - 1)],
            send_sem=b_send.at[q], recv_sem=b_recv.at[q],
            device_id={"space": peer(1)}, device_id_type=MESH,
        ).wait()
        value = own[q, pl.ds(0, heights[q]), :]
        for step in range(1, groups):
            value = value + recv_b[q][step].astype(jnp.float32)
        sums.append(value)
        for slot in range(SIZES[q]):
            final[starts[q] + slot, pl.ds(0, per), :] = value[slot * per : (slot + 1) * per]
    first = lines[0]
    norms = (
        sums[0][first : first + 1] + sums[0][first + 1 : first + 2] + sums[0][first + 2 : first + 3]
    ) / (3.0 * volume)
    lane = lax.broadcasted_iota(jnp.int32, (1, 128), 1)
    for row in range(own_rows):
        mine = jnp.sum(
            jnp.where(lane == own_rows * me + row, norms, 0.0), axis=1, keepdims=True
        )
        scale = 1.0 / (math.sqrt(3.0 * volume) * jnp.sqrt(norms * mine))
        for k in range(ncomb):
            for p in range(2):
                value = final[place[k], pl.ds(p * own_rows + row, 1), :] * scale
                out_ref[k, row, pl.ds(p, 1), :] = value[:, 0:nv]


def elementals(vectors, links, directions, momenta):
    count = lax.axis_size("space")
    _, parts, nv, depth, sites = vectors.shape
    ncomb = directions.shape[0]
    own_rows = nv // count
    groups = count // 2
    chunks = len(SIZES)
    lines = [size * 2 * own_rows + (q == 0) for q, size in enumerate(SIZES)]
    heights = [-(-(n + 2 * (q == 0)) // 8) * 8 for q, n in enumerate(lines)]
    height = max(heights)
    span = depth * 3 * sites
    fields = jnp.transpose(vectors, (3, 0, 1, 2, 4)).reshape(depth, 3, 2 * nv, sites)
    body = functools.partial(kernel, count, depth * count * sites, depth * count)
    smem = pl.BlockSpec(memory_space=pltpu.SMEM)
    vmem = pl.BlockSpec(memory_space=pltpu.VMEM)
    f32, bf16 = jnp.float32, jnp.bfloat16
    return pl.pallas_call(
        body,
        out_shape=jax.ShapeDtypeStruct((ncomb, own_rows, 2, nv), f32),
        in_specs=[vmem, vmem, smem, smem],
        out_specs=vmem,
        scratch_shapes=[
            pltpu.VMEM((2, 3, 2 * nv, sites), bf16),
            pltpu.VMEM((3, 3, 2, depth, sites), bf16),
            pltpu.VMEM((3, 18 * depth, sites), f32),
            pltpu.VMEM((2, 18 * depth, sites), f32),
            pltpu.VMEM((2, 3, 2 * nv, sites), f32),
            pltpu.VMEM((4, depth, 3, 2 * nv, sites), f32),
            pltpu.VMEM((3, ncomb * depth, sites), f32),
            pltpu.VMEM((256, span), bf16),
            pltpu.VMEM((2, nv, 128), f32),
            pltpu.VMEM((chunks, max(lines), groups, 128), f32),
            pltpu.VMEM((chunks, max(lines), groups, 128), f32),
            pltpu.VMEM((groups * height, 128), f32),
            *[pltpu.VMEM((groups, rows, 128), bf16) for rows in heights],
            *[pltpu.VMEM((groups, rows, 128), bf16) for rows in heights],
            pltpu.VMEM((chunks, height, 128), f32),
            pltpu.VMEM((chunks, max(lines), groups, 128), f32),
            pltpu.VMEM((ncomb, 8, 128), f32),
            pltpu.SemaphoreType.DMA((3,)),
            pltpu.SemaphoreType.DMA((3,)),
            pltpu.SemaphoreType.DMA((chunks,)),
            pltpu.SemaphoreType.DMA((chunks,)),
            pltpu.SemaphoreType.DMA((chunks,)),
            pltpu.SemaphoreType.DMA((chunks,)),
        ],
        compiler_params=pltpu.CompilerParams(
            collective_id=0, has_side_effects=True, vmem_limit_bytes=40 * 1024 * 1024
        ),
    )(fields, links, directions, jnp.transpose(momenta))


def local(vectors, links, directions, momenta):
    slices = [
        elementals(vectors[t], links[t], directions, momenta) for t in range(vectors.shape[0])
    ]
    stacked = jnp.transpose(jnp.stack(slices), (0, 1, 3, 2, 4))
    return lax.all_gather(stacked, "tm", axis=0, tiled=True)


def solution(mesh):
    placed = (
        P("tm", None, None, None, "space", None),
        P("tm", None, None, None, None, "space", None),
        P(),
        P(),
    )
    return jax.shard_map(
        local,
        mesh=mesh,
        in_specs=placed,
        out_specs=P(None, None, None, "space", None),
        check_vma=False,
    )
```
